32 devices in a mesh: dp: 16 (over z, y, x), head: 2 (over core).
Axes of the slice: x: 2, y: 2, z: 4, core: 2. Of those that a mesh axis runs over, the one named last changes fastest.
Arguments:
- layer_in: float32 [4096, 768], P(('dp', 'head')), may hold values from -6 to 6
- grad_out: float32 [4096, 768], P(('dp', 'head')), may hold values from -6 to 6
- w_qkv: bfloat16 [3, 768, 768], P(None, None, 'head'), may hold values from -0.21875 to 0.21875
- w_attn: bfloat16 [768, 768], P('head'), may hold values from -3 to 3
- gain_attn: float32 [768], replicated, may hold values from 0.1 to 1.9
- shift_attn: float32 [768], replicated, may hold values from -3 to 3
- gain_moe: float32 [768], replicated, may hold values from 0.1 to 1.9
- shift_moe: float32 [768], replicated, may hold values from -3 to 3
- w_router: bfloat16 [768, 32], replicated, may hold values from -0.4375 to 0.4375
- w_in: bfloat16 [32, 768, 3072], P(('dp', 'head')), may hold values from -0.21875 to 0.21875
- w_hidden: bfloat16 [32, 3072, 768], P(('dp', 'head')), may hold values from -0.109375 to 0.109375
- expert_ids: int32 [4096, 2], P(('dp', 'head')), may hold values from 0 to 31, all different within a row; in each aligned block of 128 rows (0 to 127, 128 to 255, ...) at most 12 rows name the same one
- group_ids: int32 [16], P('dp'), may hold values from 0 to 1, as said below
- frozen: int32 [32], P(('dp', 'head')), may hold values from 0 to 1, as said below
Outputs:
- layer_out: float32 [4096, 768], P(('dp', 'head'))
- grad_in: float32 [4096, 768], P(('dp', 'head'))
- grad_qkv: float32 [3, 768, 768], P(None, 'dp', 'head')
- grad_attn: float32 [12, 49152], P('head', 'dp')
- grad_gain_attn: float32 [768], P(('dp', 'head'))
- grad_shift_attn: float32 [768], P(('dp', 'head'))
- grad_gain_moe: float32 [768], P(('dp', 'head'))
- grad_shift_moe: float32 [768], P(('dp', 'head'))
- grad_router: float32 [768, 32], P(('dp', 'head'))
- grad_w_in: float32 [32, 768, 3072], P(('dp', 'head'))
- grad_w_hidden: float32 [32, 3072, 768], P(('dp', 'head'))
The draws below stay inside these ranges and needn't reach their ends.
Inputs may be any that keep to these rules, and one draw needn't show every extreme that they name: `expert_ids`: each row names two different experts. Among the 128 rows of one device no expert is named more than 12 times, a bound that some block reaches. `group_ids`: exactly half of the entries are 1. `frozen`: exactly half of the entries are 1.
All inputs are finite; a program needn't handle non-finite values.
Results may differ from the reference program's by a relative error of at most 0.012.
The reference program's roundings to bfloat16 on the way count: a program that leaves them out, or rounds other values in their place, can miss the bound.
Values may be sent and summed in bfloat16 or wider, within the bound.
A program may use at most 128 MiB of HBM per device.

```python
import math
import jax
import jax.numpy as jnp
import numpy as np
from jax import lax

D = 768
HEADS = 12
HEAD_DIM = 64
FF = 3072
TOP = 2
TOK_DEV = 128
TOKENS = 4096
GROUPS = 16
EXPERTS = 32
CAP = 12
QBLK = 256


def draw_group_ids(key, part):
    order = jax.random.permutation(jax.random.fold_in(key, 11), GROUPS)
    return (order < GROUPS // 2).astype(jnp.int32)


def draw_frozen(key, part):
    order = jax.random.permutation(jax.random.fold_in(key, 23), EXPERTS)
    return (order < EXPERTS // 2).astype(jnp.int32)


def strengthened(values, own_key, source, target, shards_of, factor):
    def block_of(position):
        return (jnp.arange(values.shape[position]) // (values.shape[position] // shards_of)).reshape((-1,) + (1,) * (values.ndim - 1 - position))

    one_side = jax.random.permutation(own_key, shards_of)[block_of(target)]
    other_side = (block_of(target) + shards_of // 2) % shards_of
    return jnp.where((block_of(source) == one_side) | (block_of(source) == other_side), factor * values, values)


def block_levels(stream_key, dims, split, least, largest):
    gain = 1.0
    for axis_at, blocks in split:
        heights = jax.random.uniform(jax.random.fold_in(jax.random.fold_in(stream_key, 6), axis_at), (blocks,), jnp.float32, least / len(split), largest / len(split))
        gain = gain * jnp.repeat(jnp.exp(heights), dims[axis_at] // blocks).reshape((-1,) + (1,) * (len(dims) - 1 - axis_at))
    return gain


def assign_block(stream_key, own, number, rows, count, top, reach, slope):
    sequence = jax.random.permutation(stream_key, count)
    packed, usual = shares(count, rows * top, reach, slope, True), shares(count, rows * top, reach, slope, False)
    places = jnp.arange(count)

    def named(lengths, turn):
        used = int((lengths > 0).sum())
        fixed = max(1, used // 4)
        moved = fixed + (places - fixed + turn * (used - fixed)) % max(1, count - fixed)
        return jnp.zeros((count,), jnp.int32).at[sequence[jnp.where(places < fixed, places, moved)]].set(jnp.asarray(lengths, jnp.int32))

    lengths = jnp.where(number % 4 == 0, named(packed, number // 4), named(usual, number - number // 4 - 1))
    mixed = jax.random.permutation(jax.random.fold_in(own, 3), count)
    donor, taker = mixed[0:count // 2 * 2:2], mixed[1:count // 2 * 2:2]
    room = jnp.minimum(lengths[donor] - 1, reach - lengths[taker]) // 2
    room = jnp.where((donor == sequence[0]) | (taker == sequence[0]) | (lengths[taker] == 0), 0, jnp.maximum(room, 0))
    moved = jax.random.randint(jax.random.fold_in(own, 4), (count // 2,), 0, 1 << 20) % (room + 1)
    lengths = lengths.at[donor].add(-moved).at[taker].add(moved)
    items = jnp.searchsorted(jnp.cumsum(lengths), jnp.arange(rows * top), side="right").astype(jnp.int32)
    table = items.reshape(top, rows).T
    table = table[jax.random.permutation(jax.random.fold_in(own, 1), rows)]
    turn = jax.random.randint(jax.random.fold_in(own, 2), (rows, 1), 0, top)
    return jnp.take_along_axis(table, (jnp.arange(top)[None, :] + turn) % top, axis=1)


def shares(number_of, total, reach, skew, full):
    loads = [(1 << 20) // math.isqrt(grade ** skew) + 1 for grade in range(1, number_of + 1)]
    largest = reach if full else min(reach, max(-(-total // number_of), total * loads[0] // sum(loads)))
    least = 1 if total - largest >= number_of - 1 else 0
    counts, spare = [largest] + [least] * (number_of - 1), total - largest - least * (number_of - 1)
    while spare > 0:
        movable = [i for i in range(1, number_of) if counts[i] < largest] or [i for i in range(1, number_of) if counts[i] < reach]
        mass, left = sum([loads[i] for i in movable]), spare
        for i in movable:
            more = min(reach - counts[i], max(1, left * loads[i] // mass), spare)
            counts[i] = counts[i] + more
            spare = spare - more
    return np.array(counts)


def gaussian(own_key, dims, scale, bound, split=(), held_as=jnp.bfloat16):
    drawn = scale * jax.random.normal(own_key, dims, jnp.float32)
    if split:
        drawn = drawn * block_levels(own_key, dims, split, -0.22, 0.18)
    return jnp.clip(drawn, -bound, bound).astype(held_as)


def noise_with(own_key, shape, width, reach, cuts, heavy, held_as=jnp.bfloat16):
    entries = width * jax.random.normal(own_key, shape, jnp.float32)
    if cuts:
        entries = entries * block_levels(own_key, shape, cuts, -0.22, 0.18)
    return jnp.clip(strengthened(entries, jax.random.fold_in(own_key, 3), *heavy), -reach, reach).astype(held_as)


def setup_inputs(seed: int = 0) -> dict:
    splits = jax.random.split(jax.random.key(seed), 15)
    layer_in = gaussian(splits[0], (TOKENS, D), 1.0, 6.0, ((0, 32),), jnp.float32)
    grad_out = noise_with(splits[1], (TOKENS, D), 1.0, 6.0, ((0, 32),), (0, 1, 32, 2.75), jnp.float32)
    w_qkv = gaussian(splits[2], (3, D, HEADS * HEAD_DIM), D ** -0.5, 0.21875, ((2, 2),))
    w_attn = gaussian(splits[3], (HEADS * HEAD_DIM, D), 4 ** -0.5, 3.0, ((0, 2),))
    gain_attn = jnp.clip(1.0 + 0.18 * jax.random.normal(splits[4], (D,), jnp.float32), 0.1, 1.9)
    shift_attn = gaussian(splits[5], (D,), 0.5, 3.0, (), jnp.float32)
    gain_moe = jnp.clip(1.0 + 0.18 * jax.random.normal(splits[6], (D,), jnp.float32), 0.1, 1.9)
    shift_moe = gaussian(splits[7], (D,), 0.5, 3.0, (), jnp.float32)
    w_router = gaussian(splits[8], (D, EXPERTS), (D // 4) ** -0.5, 0.4375)
    w_in = gaussian(splits[9], (EXPERTS, D, FF), D ** -0.5, 0.21875, ((0, 32),))
    w_hidden = gaussian(splits[10], (EXPERTS, FF, D), FF ** -0.5, 0.109375, ((0, 32),))
    expert_ids_keys = jax.random.split(jax.random.fold_in(splits[11], 1), TOKENS // TOK_DEV)
    expert_ids_turns = jax.random.permutation(jax.random.fold_in(splits[11], 3), TOKENS // TOK_DEV)
    expert_ids = jax.vmap(lambda own, number: assign_block(jax.random.fold_in(splits[11], 2), own, number, TOK_DEV, EXPERTS, TOP, CAP, 2))(expert_ids_keys, expert_ids_turns).reshape((TOKENS, TOP))
    group_ids = draw_group_ids(jax.random.fold_in(splits[14], 71), 0)
    frozen = draw_frozen(jax.random.fold_in(splits[14], 71), 0)
    return dict(layer_in=layer_in, grad_out=grad_out, w_qkv=w_qkv, w_attn=w_attn, gain_attn=gain_attn, shift_attn=shift_attn, gain_moe=gain_moe, shift_moe=shift_moe, w_router=w_router, w_in=w_in, w_hidden=w_hidden, expert_ids=expert_ids, group_ids=group_ids, frozen=frozen)


@jax.custom_vjp
def low(v):
    return lax.optimization_barrier(v.astype(jnp.bfloat16)).astype(jnp.float32)

@jax.custom_vjp
def low_back(v):
    return v

def low_keep(v):
    return (low(v), None)

def low_pass(kept, grad):
    return (grad,)

def back_keep(v):
    return (v, None)

def back_low(kept, grad):
    return (low(grad),)
low.defvjp(low_keep, low_pass)
low_back.defvjp(back_keep, back_low)
highest = lax.Precision.HIGHEST
norm_epsilon = 1e-05
masked_value = -1e+30

def layer_norm(values, gain_vec, shift_vec):
    center = values - lax.optimization_barrier(jnp.mean(values, axis=-1, keepdims=True))
    spread = lax.optimization_barrier(jnp.mean(center * center, axis=-1, keepdims=True))
    return center * lax.rsqrt(spread + norm_epsilon) * gain_vec + shift_vec

def attend_group(inputs, long_flag, w_qkv, w_attn, gain_attn, shift_attn):
    length = inputs.shape[0]
    normed = low(layer_norm(inputs, gain_attn, shift_attn))
    project = jnp.einsum('rd,tdc->trc', normed, w_qkv, precision=highest)
    project = low(low_back(project))
    queries = project[0].reshape(length, HEADS, HEAD_DIM)
    keys_all = project[1].reshape(length, HEADS, HEAD_DIM)
    values_all = project[2].reshape(length, HEADS, HEAD_DIM)
    positions = jnp.arange(length)
    half_len = length // 2
    score_scale = HEAD_DIM ** (-0.5)

    def one_block(offset):
        q_block = lax.dynamic_slice_in_dim(queries, offset, QBLK, 0)
        scores = jnp.einsum('qhc,khc->hqk', q_block, keys_all, precision=highest) * score_scale
        scores = low_back(scores)
        q_pos = offset + jnp.arange(QBLK)
        same_doc = q_pos[:, None] // half_len == positions[None, :] // half_len
        allowed = (positions[None, :] <= q_pos[:, None]) & (same_doc | (long_flag == 1))
        scores = jnp.where(allowed[None], scores, masked_value)
        weights = low(jax.nn.softmax(scores, axis=-1))
        return jnp.einsum('hqk,khc->qhc', weights, values_all, precision=highest)
    offsets = (jnp.arange(length // QBLK) * QBLK).astype(jnp.int32)
    mixed_heads = lax.map(jax.checkpoint(one_block), offsets).reshape(length, HEADS * HEAD_DIM)
    mixed_heads = low(low_back(mixed_heads))
    attn_out = low_back(jnp.dot(mixed_heads, w_attn, precision=highest))
    return inputs + attn_out

def expert_apply(member):
    slot_rows, w_first, second = member
    hidden = low_back(jnp.dot(slot_rows, w_first, precision=highest))
    activated = low(jax.nn.gelu(hidden))
    return low(low_back(jnp.dot(activated, second, precision=highest)))

def forward(layer_in, w_qkv, w_attn, gain_attn, shift_attn, gain_moe, shift_moe, w_router, w_in, w_hidden, expert_ids, group_ids):
    grouped = layer_in.reshape(GROUPS, 2 * TOK_DEV, D)

    def attend_member(member):
        return attend_group(member[0], member[1], w_qkv, w_attn, gain_attn, shift_attn)
    residual = lax.map(attend_member, (grouped, group_ids)).reshape(TOKENS, D)
    normed = low(layer_norm(residual, gain_moe, shift_moe))
    logits = low_back(jnp.dot(normed, w_router, precision=highest))
    chosen = jnp.take_along_axis(logits, expert_ids, axis=1)
    gate_probs = jax.nn.softmax(chosen, axis=-1)
    devices = TOKENS // TOK_DEV
    flat_ids = expert_ids.reshape(devices, TOK_DEV * TOP).astype(jnp.int32)
    one_hot = (flat_ids[:, :, None] == jnp.arange(EXPERTS)[None, None, :]).astype(jnp.int32)
    slot_ranks = lax.optimization_barrier(jnp.sum((jnp.cumsum(one_hot, axis=1) - 1) * one_hot, axis=-1)).astype(jnp.int32)
    sources = jnp.broadcast_to(jnp.arange(devices)[:, None], flat_ids.shape).astype(jnp.int32)
    pair_rows = jnp.repeat(normed, TOP, axis=0).reshape(devices, TOK_DEV * TOP, D)
    received = jnp.zeros((EXPERTS, devices, CAP, D), jnp.float32).at[flat_ids, sources, slot_ranks].add(pair_rows)
    received = low_back(received)
    produced = lax.map(jax.checkpoint(expert_apply), (received.reshape(EXPERTS, devices * CAP, D), w_in, w_hidden))
    produced = produced.reshape(EXPERTS, devices, CAP, D)
    picked = produced[flat_ids, sources, slot_ranks].reshape(TOKENS, TOP, D)
    return residual + lax.optimization_barrier(jnp.sum(gate_probs[:, :, None] * picked, axis=1))

def reference(layer_in, grad_out, w_qkv, w_attn, gain_attn, shift_attn, gain_moe, shift_moe, w_router, w_in, w_hidden, expert_ids, group_ids, frozen):
    floats = (layer_in, w_qkv.astype(jnp.float32), w_attn.astype(jnp.float32), gain_attn, shift_attn, gain_moe, shift_moe, w_router.astype(jnp.float32), w_in.astype(jnp.float32), w_hidden.astype(jnp.float32))

    def wrapped(*params):
        return forward(*params, expert_ids, group_ids)
    layer_out, pullback = jax.vjp(wrapped, *floats)
    gradients = pullback(grad_out)
    trainable = (1 - frozen).astype(jnp.float32)[:, None, None]
    return (layer_out, gradients[0], gradients[1], gradients[2].reshape(HEADS, HEAD_DIM * D), gradients[3], gradients[4], gradients[5], gradients[6], gradients[7], gradients[8] * trainable, gradients[9] * trainable)
```

```python
import functools

import jax
import jax.numpy as jnp
from jax import lax
from jax.experimental import pallas as pl
from jax.experimental.pallas import tpu as pltpu
from jax.sharding import PartitionSpec as P

HEAD_DIM = 64
norm_epsilon = 1e-05
masked_value = -1e30
MESH = pl.DeviceIdType.MESH
f32 = jnp.float32
bf16 = jnp.bfloat16
highest = lax.Precision.HIGHEST


def mm(a, b, dims=((1,), (0,)), precision=None):
    return lax.dot_general(a, b, (dims, ((), ())), precision=precision, preferred_element_type=f32)


NN = ((1,), (0,))
NT = ((1,), (1,))
TN = ((0,), (0,))


def iota(shape, dim):
    return lax.broadcasted_iota(jnp.int32, shape, dim)


def hat(x):
    c = x - jnp.mean(x, axis=-1, keepdims=True)
    r = lax.rsqrt(jnp.mean(c * c, axis=-1, keepdims=True) + norm_epsilon)
    return c * r, r


def norm_back(dy, x_hat, r, gain):
    dyg = dy * gain
    m1 = jnp.mean(dyg, axis=-1, keepdims=True)
    m2 = jnp.mean(dyg * x_hat, axis=-1, keepdims=True)
    return r * (dyg - m1 - x_hat * m2)


def gelu_both(x):
    k = 0.7978845608028654
    x2 = x * x
    t = jnp.tanh(k * (x + 0.044715 * x2 * x))
    half = 0.5 * (1.0 + t)
    slope = half + 0.5 * x * (1.0 - t * t) * (k * (1.0 + 0.134145 * x2))
    return x * half, slope


def layer_kernel(
    n_dp,
    n_head,
    in_hbm,
    gout_hbm,
    wqkv_hbm,
    wattn_hbm,
    gain_attn,
    shift_attn,
    gain_moe,
    shift_moe,
    wr_ref,
    win_hbm,
    whid_hbm,
    ids_ref,
    group_ref,
    lout_hbm,
    gin_hbm,
    rs_out_hbm,
    small_hbm,
    xs_hbm,
    gp_hbm,
    act_hbm,
    gh_hbm,
    x_in,
    g_out,
    wqkv,
    wattn,
    win,
    whid,
    nr,
    qkv,
    probs,
    mixed,
    apart,
    arecv,
    resid,
    sel_a,
    sel_b1,
    sel_b2,
    s_go,
    r_go,
    s_x,
    r_x,
    s_gt,
    r_gt,
    s_gr,
    r_gr,
    s_h,
    r_h,
    s_pr,
    r_pr,
    xs,
    gos,
    act,
    gh,
    grow,
    gar,
    gmix,
    gqkv,
    npart,
    nrecv,
    rsb,
    rc0,
    rc1,
    rc2,
    rc3,
    rsf,
    sm_s,
    sm_r,
    lout,
    gin,
    small,
    ld_sem,
    out_sem,
    pair_s,
    pair_r,
    a2a_s,
    a2a_r,
    rs_s,
    rs_r,
    self_sem,
):
    n = n_dp * n_head
    dp = lax.axis_index("dp")
    hd = lax.axis_index("head")
    me = dp * n_head + hd
    rows, width = x_in.shape
    length = nr.shape[0]
    ff = act.shape[1]
    experts = wr_ref.shape[1]
    wl = wattn.shape[0]
    half_w = width // 2
    packed = s_x.shape[1]

    def dev(p):
        return (p // n_head, lax.rem(p, n_head))

    loads = [
        pltpu.make_async_copy(in_hbm, x_in, ld_sem.at[0]),
        pltpu.make_async_copy(gout_hbm, g_out, ld_sem.at[1]),
        pltpu.make_async_copy(wqkv_hbm, wqkv, ld_sem.at[2]),
        pltpu.make_async_copy(wattn_hbm, wattn, ld_sem.at[3]),
        pltpu.make_async_copy(win_hbm.at[0], win, ld_sem.at[4]),
        pltpu.make_async_copy(whid_hbm.at[0], whid, ld_sem.at[5]),
    ]
    for c in loads:
        c.start()
    bar = pltpu.get_barrier_semaphore()

    def greet(i, c):
        p = lax.rem(me + i, n)
        pl.semaphore_signal(bar, inc=1, device_id=dev(p), device_id_type=MESH)
        return c

    lax.fori_loop(1, n, greet, 0)

    quarter = n // 4
    z = me // quarter
    far1 = (lax.rem(z + 2, 4) * quarter, quarter, 0)
    far2 = ((3 - z) * quarter, quarter, 1)
    near = ((z // 2) * 2 * quarter, 2 * quarter, 2)
    order = (far1, far2, near)

    def x_copy(ph, src, dst, unit, p, q):
        if unit:
            s = src.at[pl.ds(pl.multiple_of(p * unit, unit), unit)]
            d = dst.at[pl.ds(pl.multiple_of(q * unit, unit), unit)]
        else:
            s = src.at[p]
            d = dst.at[q]
        return pltpu.make_async_remote_copy(
            s, d, a2a_s.at[ph, p], a2a_r.at[ph, q], device_id=dev(p), device_id_type=MESH
        )

    def send_group(ph, src, dst, unit, group):
        base, count, _ = group

        def go(j, c):
            p = base + lax.rem(me + j, count)

            @pl.when(p != me)
            def _():
                x_copy(ph, src, dst, unit, p, me).start()

            return c

        lax.fori_loop(0, count, go, 0)

    def wait_group(ph, src, dst, unit, group):
        base, count, _ = group

        def go(j, c):
            p = base + lax.rem(me + j, count)

            @pl.when(p != me)
            def _():
                x_copy(ph, src, dst, unit, p, p).wait_recv()

            return c

        lax.fori_loop(0, count, go, 0)

    def drain(ph, src, dst, unit):
        def go(i, c):
            p = lax.rem(me + i, n)
            x_copy(ph, src, dst, unit, p, me).wait_send()
            return c

        lax.fori_loop(1, n, go, 0)

    def self_copy(ph, src, dst, unit):
        if unit:
            at = pl.ds(pl.multiple_of(me * unit, unit), unit)
        else:
            at = me
        return pltpu.make_async_copy(src.at[at], dst.at[at], self_sem.at[ph])

    def pair_copy(k, src, dst):
        return pltpu.make_async_remote_copy(
            src, dst, pair_s.at[k], pair_r.at[k], device_id=(dp, 1 - hd), device_id_type=MESH
        )

    mine = pl.ds(pl.multiple_of(hd * rows, rows), rows)
    other = pl.ds(pl.multiple_of((1 - hd) * rows, rows), rows)

    lane_e = iota((rows, experts), 1)
    hits = [jnp.where(lane_e == ids_ref[:, k : k + 1], 1.0, 0.0) for k in range(2)]
    below = jnp.where(iota((rows, rows), 0) > iota((rows, rows), 1), 1.0, 0.0).astype(bf16)
    before = mm(below, (hits[0] + hits[1]).astype(bf16))
    ranks = [jnp.sum(before * hits[k], axis=1, keepdims=True) for k in range(2)]
    col = iota((rows, 8 * n), 1).astype(f32)
    for k in range(2):
        first = 8.0 * ids_ref[:, k : k + 1].astype(f32)
        rk = ranks[k]
        sel_a[k] = jnp.where((rk < 8.0) & (col == first + rk), 1.0, 0.0).astype(bf16)
        sel_b1[k] = jnp.where((rk >= 8.0) & (col == first + rk - 8.0), 1.0, 0.0).astype(bf16)
        sel_b2[k] = jnp.where((rk >= 8.0) & (col == first + rk - 4.0), 1.0, 0.0).astype(bf16)

    def spread(block, dst):
        dst[:, :width] = mm(sel_a[0] + sel_a[1], block, TN).astype(bf16)
        dst[:, width:] = (
            mm(sel_b1[0] + sel_b1[1], block[:, :half_w], TN)
            + mm(sel_b2[0] + sel_b2[1], block[:, half_w:], TN)
        ).astype(bf16)

    def collect(src, k):
        if k is None:
            a, b1, b2 = (s[0] + s[1] for s in (sel_a, sel_b1, sel_b2))
        else:
            a, b1, b2 = sel_a[k], sel_b1[k], sel_b2[k]
        tail = src[:, width:]
        return mm(a, src[:, :width]) + jnp.concatenate([mm(b1, tail), mm(b2, tail)], axis=1)

    loads[0].wait()
    x_hat, _ = hat(x_in[...])
    nr[mine] = (x_hat * gain_attn[...] + shift_attn[...]).astype(bf16)
    loads[1].wait()
    spread(g_out[...].astype(bf16), s_go)
    pl.semaphore_wait(bar, n - 1)
    gather = pair_copy(0, nr.at[mine], nr.at[mine])
    gather.start()
    for group in order:
        send_group(0, s_go, r_go, 8, group)
    self_copy(0, s_go, r_go, 8).start()

    loads[2].wait()
    gather.wait()
    for t in range(3):
        qkv[t] = mm(nr[...], wqkv[t]).astype(bf16)
    long_flag = group_ref[0]
    scale = HEAD_DIM ** (-0.5)
    lane = iota((length, 2 * HEAD_DIM), 1)
    lows = [lane < HEAD_DIM, lane >= HEAD_DIM]
    q_pos = iota((length, length), 0)
    k_pos = iota((length, length), 1)
    same = (q_pos < length // 2) == (k_pos < length // 2)
    bias = jnp.where(
        (k_pos <= q_pos) & (same | (long_flag == 1)), 0.0, masked_value
    )

    def attend(j, c):
        cols = pl.ds(pl.multiple_of(j * 128, 128), 128)
        q, k, v = qkv[0, :, cols], qkv[1, :, cols], qkv[2, :, cols]
        outs = []
        for s in range(2):
            sc = mm(jnp.where(lows[s], q, jnp.zeros_like(q)), k, NT) * scale
            sc = jnp.where(bias == 0.0, sc, masked_value)
            e = jnp.exp(sc - jnp.max(sc, axis=-1, keepdims=True))
            p = e / jnp.sum(e, axis=-1, keepdims=True)
            probs[2 * j + s] = p
            outs.append(mm(p.astype(bf16), v))
        mixed[:, cols] = jnp.where(lows[0], outs[0], outs[1]).astype(bf16)
        return c

    lax.fori_loop(0, wl // 128, attend, 0)
    loads[3].wait()
    apart[...] = mm(mixed[other, :], wattn[...])
    half_sum = pair_copy(1, apart, arecv)
    half_sum.start()
    own = mm(mixed[mine, :], wattn[...]) + x_in[...]
    half_sum.wait()
    resid[...] = own + arecv[...]
    y_hat, _ = hat(resid[...])
    low = (y_hat * gain_moe[...] + shift_moe[...]).astype(bf16)
    spread(low, s_x)
    for group in order:
        send_group(1, s_x, r_x, 8, group)
    self_copy(1, s_x, r_x, 8).start()
    logits = mm(low, wr_ref[...])
    chosen = [jnp.sum(logits * hits[k], axis=1, keepdims=True) for k in range(2)]
    top = jnp.maximum(chosen[0], chosen[1])
    exps = [jnp.exp(c - top) for c in chosen]
    gates = [e / (exps[0] + exps[1]) for e in exps]
    lane128 = iota((rows, 128), 1).astype(f32)
    marks = [jnp.where(lane128 == ranks[k], 1.0, 0.0) for k in range(2)]
    s_gt[:, 0, :] = mm(hits[0], gates[0] * marks[0], TN, highest) + mm(
        hits[1], gates[1] * marks[1], TN, highest
    )
    for group in order:
        send_group(2, s_gt, r_gt, 0, group)
    self_copy(2, s_gt, r_gt, 0).start()

    loads[4].wait()
    loads[5].wait()
    fb = 512
    starts = (0, 12 * quarter, 24 * quarter)
    self_copy(0, s_go, r_go, 8).wait()
    self_copy(1, s_x, r_x, 8).wait()
    self_copy(2, s_gt, r_gt, 0).wait()
    for base, count, which in (near, far1, far2):
        group = (base, count, which)
        m = 12 * count
        at = starts[which]
        for ph, s, d, u in ((0, s_go, r_go, 8), (2, s_gt, r_gt, 0), (1, s_x, r_x, 8)):
            wait_group(ph, s, d, u, group)
        blk = pl.ds(pl.multiple_of(base * 8, 8 * count), 8 * count)
        r4 = iota((4 * count, 8 * count), 0)
        c8 = iota((4 * count, 8 * count), 1)
        hit = (r4 // 4) == (c8 // 8)
        p1 = jnp.where(hit & ((r4 % 4) == (c8 % 8)), 1.0, 0.0).astype(bf16)
        p2 = jnp.where(hit & ((r4 % 4) + 4 == (c8 % 8)), 1.0, 0.0).astype(bf16)
        for src, dst in ((r_x, xs), (r_go, gos)):
            dst[at : at + 8 * count] = src[blk, :width]
            tail = src[blk, width:]
            dst[at + 8 * count : at + m] = jnp.concatenate(
                [mm(p1, tail).astype(bf16), mm(p2, tail).astype(bf16)], axis=1
            )
        rr = iota((m, count), 0)
        source_of = jnp.where(rr < 8 * count, rr // 8, (rr - 8 * count) // 4)
        e_of = jnp.where(source_of == iota((m, count), 1), 1.0, 0.0)
        rl = iota((m, 128), 0)
        lane_of = jnp.where(rl < 8 * count, rl % 8, 8 + (rl - 8 * count) % 4)
        l_of = jnp.where(lane_of == iota((m, 128), 1), 1.0, 0.0)
        gate = jnp.sum(
            mm(e_of, r_gt[pl.ds(base, count), 0, :], NN, highest) * l_of, axis=1, keepdims=True
        )
        rows_m = slice(at, at + m)
        gos[rows_m] = (gos[rows_m].astype(f32) * gate).astype(bf16)

        def up(j, acc):
            cols = pl.ds(pl.multiple_of(j * fb, fb), fb)
            hidden = mm(xs[rows_m], win[:, cols])
            a, slope = gelu_both(hidden)
            a = a.astype(bf16)
            act[rows_m, cols] = a
            ga = mm(gos[rows_m], whid[cols, :], NT)
            gh[rows_m, cols] = (slope * ga).astype(bf16)
            prod = ga * a.astype(f32)
            for q in range(fb // 128):
                acc = acc + prod[:, 128 * q : 128 * q + 128]
            return acc

        dot_sum = lax.fori_loop(0, ff // fb, up, jnp.zeros((m, 128), f32))
        dots = jnp.sum(dot_sum, axis=1, keepdims=True)
        s_h[pl.ds(base, count), 0, :] = mm(e_of, dots * l_of, TN, highest)

        def back(j, c):
            cols = pl.ds(pl.multiple_of(j * 256, 256), 256)
            grow[rows_m, cols] = mm(gh[rows_m, :], win[cols, :], NT).astype(bf16)
            return c

        lax.fori_loop(0, width // 256, back, 0)
        s_gr[blk, :width] = grow[at : at + 8 * count]
        tail = grow[at + 8 * count : at + m]
        s_gr[blk, width:] = (
            mm(p1, tail[:, :half_w], TN) + mm(p2, tail[:, half_w:], TN)
        ).astype(bf16)
        send_group(3, s_gr, r_gr, 8, group)
        send_group(4, s_h, r_h, 0, group)

    self_copy(3, s_gr, r_gr, 8).start()
    self_copy(4, s_h, r_h, 0).start()
    outs = [
        pltpu.make_async_copy(xs, xs_hbm, out_sem.at[0]),
        pltpu.make_async_copy(gos, gp_hbm, out_sem.at[1]),
        pltpu.make_async_copy(act, act_hbm, out_sem.at[2]),
        pltpu.make_async_copy(gh, gh_hbm, out_sem.at[3]),
    ]
    for c in outs:
        c.start()

    self_copy(3, s_gr, r_gr, 8).wait()

    def down(j, c):
        cols = pl.ds(pl.multiple_of(j * 256, 256), 256)
        grow[:, cols] = mm(act[...], whid[:, cols]).astype(bf16)
        return c

    lax.fori_loop(0, width // 256, down, 0)
    for base, count, which in order:
        m = 12 * count
        at = starts[which]
        blk = pl.ds(pl.multiple_of(base * 8, 8 * count), 8 * count)
        r4 = iota((4 * count, 8 * count), 0)
        c8 = iota((4 * count, 8 * count), 1)
        hit = (r4 // 4) == (c8 // 8)
        p1 = jnp.where(hit & ((r4 % 4) == (c8 % 8)), 1.0, 0.0).astype(bf16)
        p2 = jnp.where(hit & ((r4 % 4) + 4 == (c8 % 8)), 1.0, 0.0).astype(bf16)
        s_pr[blk, :width] = grow[at : at + 8 * count]
        tail = grow[at + 8 * count : at + m]
        s_pr[blk, width:] = (
            mm(p1, tail[:, :half_w], TN) + mm(p2, tail[:, half_w:], TN)
        ).astype(bf16)
        send_group(5, s_pr, r_pr, 8, (base, count, which))
    self_copy(5, s_pr, r_pr, 8).start()

    self_copy(4, s_h, r_h, 0).wait()
    for group in order:
        wait_group(4, s_h, r_h, 0, group)
        wait_group(3, s_gr, r_gr, 8, group)
    y_hat, y_r = hat(resid[...])
    low = (y_hat * gain_moe[...] + shift_moe[...]).astype(bf16)
    back_rows = r_h[:, 0, :]
    dots = [jnp.sum(mm(hits[k], back_rows, NN, highest) * marks[k], axis=1, keepdims=True) for k in range(2)]
    both = dots[0] + dots[1]
    g_logits = ((dots[0] - gates[0] * both) * hits[0] + (dots[1] - gates[1] * both) * hits[1]).astype(bf16)
    g_norm = collect(r_gr, None) + mm(g_logits, wr_ref[...], NT)
    g_res = g_out[...] + norm_back(g_norm, y_hat, y_r, gain_moe[...])
    gar[mine] = g_res.astype(bf16)
    share = pair_copy(2, gar.at[mine], gar.at[mine])
    share.start()
    gin[...] = g_res
    col_rows = mm(g_logits, low, TN)
    moe_gain = jnp.sum(g_norm * y_hat, axis=0, keepdims=True)
    moe_shift = jnp.sum(g_norm, axis=0, keepdims=True)
    share.wait()

    gmix[...] = mm(gar[...], wattn[...], NT).astype(bf16)
    own_rows = HEAD_DIM // n_dp
    n_loc = wl // HEAD_DIM
    per = 2 * own_rows * n_loc
    ci = iota((wl, n_dp * per), 1)
    ri = iota((wl, n_dp * per), 0)
    within = ci % per
    row_r = (within // n_loc) % own_rows
    want = (within % n_loc) * HEAD_DIM + (ci // per) * own_rows + row_r
    pick = jnp.where(ri == want, 1.0, 0.0).astype(bf16)
    mixed_p = mm(mixed[...], pick).astype(bf16)
    block_shape = (2,) * 4 + (per, half_w)

    def rs_put(t, val):
        rsb[t] = val.astype(bf16).reshape(block_shape)

    left = (iota((n_dp * per, half_w), 0) % per) < per // 2
    rs_put(
        3,
        jnp.where(
            left, mm(mixed_p, gar[:, :half_w], TN), mm(mixed_p, gar[:, half_w:], TN)
        ),
    )

    bit_of = [lax.rem(dp // (1 << b), 2) for b in range(4)]
    orders = ((0, 1, 2, 3), (1, 0, 2, 3), (2, 0, 1, 3), (1, 2, 0, 3))
    stage_bufs = (rc0, rc1, rc2, rc3)

    def rs_index(t, s, flip):
        idx = [slice(None)] * 4
        for b in orders[t][:s]:
            idx[3 - b] = bit_of[b]
        b = orders[t][s]
        idx[3 - b] = 1 - bit_of[b] if flip else bit_of[b]
        return (t, *idx)

    def rs_copy(t, s):
        b = orders[t][s]
        partner = dp + (1 - 2 * bit_of[b]) * (1 << b)
        return pltpu.make_async_remote_copy(
            rsb.at[rs_index(t, s, True)],
            stage_bufs[s].at[t],
            rs_s.at[t, s],
            rs_r.at[t, s],
            device_id=(partner, hd),
            device_id_type=MESH,
        )

    rs_copy(3, 0).start()

    def attend_back(j, c):
        cols = pl.ds(pl.multiple_of(j * 128, 128), 128)
        q, k, v = qkv[0, :, cols], qkv[1, :, cols], qkv[2, :, cols]
        gm = gmix[:, cols]
        gq, gk, gv = [], [], []
        for s in range(2):
            p = probs[2 * j + s]
            gpr = mm(jnp.where(lows[s], gm, jnp.zeros_like(gm)), v, NT)
            ds = (p * (gpr - jnp.sum(p * gpr, axis=-1, keepdims=True))).astype(bf16)
            gv.append(mm(p.astype(bf16), gm, TN))
            gq.append(mm(ds, k) * scale)
            gk.append(mm(ds, q, TN) * scale)
        for t, g in enumerate((gq, gk, gv)):
            gqkv[t, :, cols] = jnp.where(lows[0], g[0], g[1]).astype(bf16)
        return c

    lax.fori_loop(0, wl // 128, attend_back, 0)
    for t in (2, 0, 1):
        rs_put(t, mm(nr[...], gqkv[t], TN))
        rs_copy(t, 0).start()

    def to_rows(at):
        return (
            mm(gqkv[0, at, :], wqkv[0], NT)
            + mm(gqkv[1, at, :], wqkv[1], NT)
            + mm(gqkv[2, at, :], wqkv[2], NT)
        )

    npart[...] = to_rows(other).astype(bf16)
    half_sum = pair_copy(3, npart, nrecv)
    half_sum.start()
    g_norm = to_rows(mine)
    half_sum.wait()
    g_norm = g_norm + nrecv[...].astype(f32)
    x_hat, x_r = hat(x_in[...])
    gin[...] = gin[...] + norm_back(g_norm, x_hat, x_r, gain_attn[...])
    vec = jnp.concatenate(
        [
            col_rows,
            jnp.sum(g_norm * x_hat, axis=0, keepdims=True),
            jnp.sum(g_norm, axis=0, keepdims=True),
            moe_gain,
            moe_shift,
            jnp.zeros((128 - experts - 4, width), f32),
        ],
        axis=0,
    )
    tall = vec.T.reshape(n, width // n // 8, 8, 128)
    packed_small = tall[:, 0]
    for j in range(1, width // n // 8):
        packed_small = packed_small + pltpu.roll(tall[:, j].reshape(8 * n, 128), 40 * j, 1).reshape(n, 8, 128)
    sm_s[...] = packed_small.reshape(8 * n, 128)
    for group in order:
        send_group(6, sm_s, sm_r, 8, group)
    self_copy(6, sm_s, sm_r, 8).start()

    for s in range(4):
        for t in (3, 2, 0, 1):
            rs_copy(t, s).wait()
            at = rs_index(t, s, False)
            total = rsb[at].astype(f32) + stage_bufs[s][t].astype(f32)
            if s < 3:
                rsb[at] = total.astype(bf16)
                rs_copy(t, s + 1).start()
            else:
                rsf[t] = total

    self_copy(5, s_pr, r_pr, 8).wait()
    for group in order:
        wait_group(5, s_pr, r_pr, 8, group)
    lout[...] = resid[...] + (gates[0] * collect(r_pr, 0) + gates[1] * collect(r_pr, 1))
    self_copy(6, sm_s, sm_r, 8).wait()
    for group in order:
        wait_group(6, sm_s, sm_r, 8, group)
    small[...] = jnp.sum(sm_r[...].reshape(n, 8, 128), axis=0)
    finals = [
        pltpu.make_async_copy(lout, lout_hbm, out_sem.at[4]),
        pltpu.make_async_copy(gin, gin_hbm, out_sem.at[5]),
        pltpu.make_async_copy(rsf, rs_out_hbm, out_sem.at[6]),
        pltpu.make_async_copy(small, small_hbm, out_sem.at[7]),
    ]
    for c in finals:
        c.start()
    for ph, s, d, u in (
        (0, s_go, r_go, 8),
        (1, s_x, r_x, 8),
        (2, s_gt, r_gt, 0),
        (3, s_gr, r_gr, 8),
        (4, s_h, r_h, 0),
        (5, s_pr, r_pr, 8),
        (6, sm_s, sm_r, 8),
    ):
        drain(ph, s, d, u)
    for c in outs + finals:
        c.wait()


def finish_kernel(
    xs, gp, act, gh, frozen, lout_i, gin_i, rs_i, small_i, g_in, g_hid, lout, gin, gqkv, gattn, router, vecs
):
    train = (1 - frozen[0]).astype(f32)
    g_in[0] = mm(xs[...], gh[...], TN) * train
    g_hid[0] = mm(act[...], gp[...], TN) * train

    @pl.when(pl.program_id(0) == 0)
    def _():
        lout[...] = lout_i[...]
        gin[...] = gin_i[...]
        for t in range(3):
            gqkv[t] = rs_i[t]
        n_loc = gattn.shape[0]
        per, half_w = rs_i.shape[1:]
        own_rows = per // 2 // n_loc
        for r in range(own_rows):
            for c in range(2):
                first = (c * own_rows + r) * n_loc
                gattn[:, (2 * r + c) * half_w : (2 * r + c + 1) * half_w] = rs_i[3, first : first + n_loc, :]
        rows = router.shape[0]
        parts = jnp.concatenate([small_i[:, 40 * j : 40 * j + 40] for j in range(rows // 8)], axis=0)
        router[...] = parts[:, : router.shape[1]]
        vecs[...] = parts[:, router.shape[1] :]


def fast_body(
    n_dp,
    n_head,
    layer_in,
    grad_out,
    w_qkv,
    w_attn,
    gain_attn,
    shift_attn,
    gain_moe,
    shift_moe,
    w_router,
    w_in,
    w_hidden,
    expert_ids,
    group_ids,
    frozen,
):
    n = n_dp * n_head
    rows, width = layer_in.shape
    wl = w_attn.shape[0]
    heads = wl // HEAD_DIM
    experts = w_router.shape[1]
    ff = w_in.shape[2]
    length = rows * n_head
    half_w = width // 2
    packed = width + half_w
    per = width // n_dp
    pairs = 12 * n
    sds = jax.ShapeDtypeStruct
    any_space = pl.BlockSpec(memory_space=pl.ANY)
    vmem = pl.BlockSpec(memory_space=pltpu.VMEM)
    V = pltpu.VMEM
    wide = V((8 * n, packed), bf16)
    thin = V((n, 1, 128), f32)
    dma = pltpu.SemaphoreType.DMA
    out = pl.pallas_call(
        functools.partial(layer_kernel, n_dp, n_head),
        out_shape=(
            sds((rows, width), f32),
            sds((rows, width), f32),
            sds((4, per, half_w), f32),
            sds((8, 128), f32),
            sds((pairs, width), bf16),
            sds((pairs, width), bf16),
            sds((pairs, ff), bf16),
            sds((pairs, ff), bf16),
        ),
        in_specs=[any_space] * 4 + [vmem] * 5 + [any_space] * 2 + [vmem, pl.BlockSpec(memory_space=pltpu.SMEM)],
        out_specs=(any_space,) * 8,
        scratch_shapes=[
            V((rows, width), f32),
            V((rows, width), f32),
            V((3, width, wl), bf16),
            V((wl, width), bf16),
            V((width, ff), bf16),
            V((ff, width), bf16),
            V((length, width), bf16),
            V((3, length, wl), bf16),
            V((heads, length, length), f32),
            V((length, wl), bf16),
            V((rows, width), f32),
            V((rows, width), f32),
            V((rows, width), f32),
            V((2, rows, 8 * n), bf16),
            V((2, rows, 8 * n), bf16),
            V((2, rows, 8 * n), bf16),
            wide,
            wide,
            wide,
            wide,
            thin,
            thin,
            wide,
            wide,
            thin,
            thin,
            wide,
            wide,
            V((pairs, width), bf16),
            V((pairs, width), bf16),
            V((pairs, ff), bf16),
            V((pairs, ff), bf16),
            V((pairs, width), bf16),
            V((length, width), bf16),
            V((length, wl), bf16),
            V((3, length, wl), bf16),
            V((rows, width), bf16),
            V((rows, width), bf16),
            V((4, 2, 2, 2, 2, per, half_w), bf16),
            V((4, 2, 2, 2, per, half_w), bf16),
            V((4, 2, 2, per, half_w), bf16),
            V((4, 2, per, half_w), bf16),
            V((4, per, half_w), bf16),
            V((4, per, half_w), f32),
            V((8 * n, 128), f32),
            V((8 * n, 128), f32),
            V((rows, width), f32),
            V((rows, width), f32),
            V((8, 128), f32),
            dma((6,)),
            dma((8,)),
            dma((4,)),
            dma((4,)),
            dma((7, n)),
            dma((7, n)),
            dma((4, 4)),
            dma((4, 4)),
            dma((7,)),
        ],
        compiler_params=pltpu.CompilerParams(
            collective_id=0, has_side_effects=True, vmem_limit_bytes=60 << 20
        ),
        name="layer",
    )(
        layer_in,
        grad_out,
        w_qkv,
        w_attn,
        gain_attn[None],
        shift_attn[None],
        gain_moe[None],
        shift_moe[None],
        w_router,
        w_in,
        w_hidden,
        expert_ids,
        group_ids,
    )
    lout, gin, rs, small, xs, gp, act, gh = out
    fb = 256
    whole = lambda *s: pl.BlockSpec(s, lambda j: (0,) * len(s))
    res = pl.pallas_call(
        finish_kernel,
        grid=(ff // fb,),
        out_shape=(
            sds((1, width, ff), f32),
            sds((1, ff, width), f32),
            sds((rows, width), f32),
            sds((rows, width), f32),
            sds((3, per, wl), f32),
            sds((heads, HEAD_DIM // n_dp * width), f32),
            sds((width // n, experts), f32),
            sds((width // n, 8), f32),
        ),
        in_specs=[
            whole(pairs, width),
            whole(pairs, width),
            pl.BlockSpec((pairs, fb), lambda j: (0, j)),
            pl.BlockSpec((pairs, fb), lambda j: (0, j)),
            pl.BlockSpec(memory_space=pltpu.SMEM),
            whole(rows, width),
            whole(rows, width),
            whole(4, per, half_w),
            whole(8, 128),
        ],
        out_specs=(
            pl.BlockSpec((1, width, fb), lambda j: (0, 0, j)),
            pl.BlockSpec((1, fb, width), lambda j: (0, j, 0)),
            whole(rows, width),
            whole(rows, width),
            whole(3, per, wl),
            whole(heads, HEAD_DIM // n_dp * width),
            whole(width // n, experts),
            whole(width // n, 8),
        ),
        compiler_params=pltpu.CompilerParams(vmem_limit_bytes=48 << 20),
        name="finish",
    )(xs, gp, act, gh, frozen, lout, gin, rs, small)
    g_in, g_hid, lout, gin, gqkv, gattn, router, vecs = res
    return (lout, gin, gqkv, gattn, vecs[:, 0], vecs[:, 1], vecs[:, 2], vecs[:, 3], router, g_in, g_hid)


def in_blocks(x, dim, size):
    before, after = (x.shape[:dim], x.shape[dim + 1 :])
    return jnp.moveaxis(x.reshape(*before, size, -1, *after), dim, 0)


def sum_at_owner(x, axis, dim):
    blocks = in_blocks(x, dim, lax.axis_size(axis))
    arrived = lax.all_to_all(blocks, axis, split_axis=0, concat_axis=0, tiled=True)
    return arrived.astype(jnp.float32).sum(axis=0)


def layer_norm(values, gain_vec, shift_vec):
    center = values - jnp.mean(values, axis=-1, keepdims=True)
    spread = jnp.mean(center * center, axis=-1, keepdims=True)
    return center * lax.rsqrt(spread + norm_epsilon) * gain_vec + shift_vec


def causal_mask(offset, q_rows, length, long_flag):
    q_pos = offset + jnp.arange(q_rows)
    k_pos = jnp.arange(length)
    half_len = length // 2
    same_doc = q_pos[:, None] // half_len == k_pos[None, :] // half_len
    return (k_pos[None, :] <= q_pos[:, None]) & (same_doc | (long_flag == 1))


def body(
    layer_in,
    grad_out,
    w_qkv,
    w_attn,
    gain_attn,
    shift_attn,
    gain_moe,
    shift_moe,
    w_router,
    w_in,
    w_hidden,
    expert_ids,
    group_ids,
    frozen,
):
    rows_dev = layer_in.shape[0]
    width = layer_in.shape[1]
    width_local = w_attn.shape[0]
    head_count = width_local // HEAD_DIM
    experts = w_router.shape[1]
    capacity = max(2, 3 * rows_dev // experts)
    long_flag = group_ids[0]
    score_scale = HEAD_DIM ** (-0.5)
    normed_attn, norm_attn_pull = jax.vjp(layer_norm, layer_in, gain_attn, shift_attn)
    normed_rows = lax.all_gather(normed_attn.astype(jnp.bfloat16), "head", axis=0, tiled=True)
    length = normed_rows.shape[0]
    q_rows = min(512, length)
    project = jnp.einsum(
        "rd,tdc->trc", normed_rows, w_qkv, preferred_element_type=jnp.float32
    ).astype(jnp.bfloat16)
    queries = project[0].reshape(length, head_count, HEAD_DIM)
    keys_all = project[1].reshape(length, head_count, HEAD_DIM)
    values_all = project[2].reshape(length, head_count, HEAD_DIM)

    def block_scores(offset):
        scores = (
            jnp.einsum("qhc,khc->hqk", queries, keys_all, preferred_element_type=jnp.float32)
            * score_scale
        )
        allowed = causal_mask(offset, q_rows, length, long_flag)
        return jnp.where(allowed[None], scores, masked_value)

    block_starts = list(range(0, length, q_rows))
    mixed_parts = []
    log_sums = []
    for offset in block_starts:
        scores = block_scores(offset)
        top_score = jnp.max(scores, axis=-1, keepdims=True)
        exp_scores = jnp.exp(scores - top_score)
        totals = jnp.sum(exp_scores, axis=-1, keepdims=True)
        probs = (exp_scores / totals).astype(jnp.bfloat16)
        log_sums.append(top_score + jnp.log(totals))
        mixed_parts.append(
            jnp.einsum("hqk,khc->qhc", probs, values_all, preferred_element_type=jnp.float32)
        )
    mixed_heads = mixed_parts[0].reshape(length, width_local).astype(jnp.bfloat16)
    attn_out = lax.psum_scatter(
        jnp.dot(mixed_heads, w_attn, preferred_element_type=jnp.float32),
        "head",
        scatter_dimension=0,
        tiled=True,
    )
    residual = layer_in + attn_out
    normed_moe, norm_moe_pull = jax.vjp(layer_norm, residual, gain_moe, shift_moe)
    moe_low = normed_moe.astype(jnp.bfloat16)
    logits = jnp.dot(moe_low, w_router, preferred_element_type=jnp.float32)
    selector = (expert_ids[:, :, None] == jnp.arange(experts)[None, None, :]).astype(jnp.float32)
    chosen = jnp.sum(logits[:, None, :] * selector, axis=-1)
    gate_probs = jax.nn.softmax(chosen, axis=-1)
    flat_ids = expert_ids.reshape(-1)
    one_hot = (flat_ids[:, None] == jnp.arange(experts)[None, :]).astype(jnp.int32)
    slot_ranks = jnp.sum((jnp.cumsum(one_hot, axis=0) - 1) * one_hot, axis=-1)
    slot_index = flat_ids * capacity + slot_ranks
    dispatch = (slot_index[:, None] == jnp.arange(experts * capacity)[None, :]).astype(jnp.bfloat16)
    dispatch = dispatch.reshape(rows_dev, expert_ids.shape[1], experts * capacity)
    send_rows = jnp.einsum("tkm,td->md", dispatch, moe_low, preferred_element_type=jnp.float32)
    send_rows = send_rows.astype(jnp.bfloat16).reshape(experts, capacity, width)
    w_first = w_in[0]
    w_second = w_hidden[0]
    slot_rows = lax.all_to_all(send_rows, ("dp", "head"), split_axis=0, concat_axis=0, tiled=True)
    hidden = jnp.einsum("sid,df->sif", slot_rows, w_first, preferred_element_type=jnp.float32)
    activated = jax.nn.gelu(hidden).astype(jnp.bfloat16)
    produced = jnp.einsum(
        "sif,fd->sid", activated, w_second, preferred_element_type=jnp.float32
    ).astype(jnp.bfloat16)
    produced, hidden, arrived = (produced, hidden, slot_rows)
    returned = lax.all_to_all(produced, ("dp", "head"), split_axis=0, concat_axis=0, tiled=True)
    picked = jnp.einsum(
        "tkm,md->tkd",
        dispatch,
        returned.reshape(experts * capacity, width),
        preferred_element_type=jnp.float32,
    )
    layer_out = residual + jnp.sum(gate_probs[:, :, None] * picked, axis=1)
    grad_gates = jnp.sum(picked * grad_out[:, None, :], axis=-1)
    grad_pair = (gate_probs[:, :, None] * grad_out[:, None, :]).astype(jnp.bfloat16)
    grad_slots = jnp.einsum("tkm,tkd->md", dispatch, grad_pair, preferred_element_type=jnp.float32)
    grad_slots = grad_slots.astype(jnp.bfloat16).reshape(experts, capacity, width)
    grad_arrived = lax.all_to_all(
        grad_slots, ("dp", "head"), split_axis=0, concat_axis=0, tiled=True
    )
    activated_full, gelu_pull = jax.vjp(jax.nn.gelu, hidden)
    activated = activated_full.astype(jnp.bfloat16)
    grad_act = jnp.einsum("sid,fd->sif", grad_arrived, w_second, preferred_element_type=jnp.float32)
    grad_hidden = gelu_pull(grad_act)[0].astype(jnp.bfloat16)
    trainable = (1 - frozen[0]).astype(jnp.float32)
    grad_w_hidden = (
        jnp.einsum("sif,sid->fd", activated, grad_arrived, preferred_element_type=jnp.float32)
        * trainable
    )[None]
    grad_w_in = (
        jnp.einsum("sid,sif->df", arrived, grad_hidden, preferred_element_type=jnp.float32)
        * trainable
    )[None]
    grad_rows = jnp.einsum(
        "sif,df->sid", grad_hidden, w_first, preferred_element_type=jnp.float32
    ).astype(jnp.bfloat16)
    grad_send = lax.all_to_all(grad_rows, ("dp", "head"), split_axis=0, concat_axis=0, tiled=True)
    grad_normed = jnp.einsum(
        "tkm,md->td",
        dispatch,
        grad_send.reshape(experts * capacity, width),
        preferred_element_type=jnp.float32,
    )
    grad_chosen = gate_probs * (
        grad_gates - jnp.sum(gate_probs * grad_gates, axis=-1, keepdims=True)
    )
    grad_logits = jnp.sum(selector * grad_chosen[:, :, None], axis=1).astype(jnp.bfloat16)
    grad_normed = grad_normed + jnp.einsum(
        "te,de->td", grad_logits, w_router, preferred_element_type=jnp.float32
    )
    grad_router = jnp.einsum("td,te->de", moe_low, grad_logits, preferred_element_type=jnp.float32)
    grad_resid_norm, grad_gain_moe, grad_shift_moe = norm_moe_pull(grad_normed)
    grad_resid = grad_out + grad_resid_norm
    grad_attn_rows = lax.all_gather(grad_resid.astype(jnp.bfloat16), "head", axis=0, tiled=True)
    grad_mixed = jnp.einsum("rd,cd->rc", grad_attn_rows, w_attn, preferred_element_type=jnp.float32)
    grad_mixed = grad_mixed.astype(jnp.bfloat16).reshape(length, head_count, HEAD_DIM)
    grad_w_attn = jnp.einsum(
        "rc,rd->cd", mixed_heads, grad_attn_rows, preferred_element_type=jnp.float32
    )
    grad_keys = jnp.zeros((length, head_count, HEAD_DIM), jnp.float32)
    grad_values = jnp.zeros((length, head_count, HEAD_DIM), jnp.float32)
    grad_query_parts = []
    for number, offset in enumerate(block_starts):
        scores = block_scores(offset)
        probs = jnp.exp(scores - log_sums[number])
        probs_low = probs.astype(jnp.bfloat16)
        grad_values = jnp.einsum(
            "hqk,qhc->khc", probs_low, grad_mixed, preferred_element_type=jnp.float32
        )
        grad_probs = jnp.einsum(
            "qhc,khc->hqk", grad_mixed, values_all, preferred_element_type=jnp.float32
        )
        grad_scores = probs * (grad_probs - jnp.sum(probs * grad_probs, axis=-1, keepdims=True))
        grad_scores = grad_scores.astype(jnp.bfloat16)
        grad_query_parts.append(
            jnp.einsum("hqk,khc->qhc", grad_scores, keys_all, preferred_element_type=jnp.float32)
            * score_scale
        )
        grad_keys = (
            jnp.einsum("hqk,qhc->khc", grad_scores, queries, preferred_element_type=jnp.float32)
            * score_scale
        )
    grad_queries = grad_query_parts[0]
    grad_project = (
        jnp.stack([grad_queries, grad_keys, grad_values])
        .reshape(3, length, width_local)
        .astype(jnp.bfloat16)
    )
    grad_w_qkv = jnp.einsum(
        "rd,trc->tdc", normed_rows, grad_project, preferred_element_type=jnp.float32
    )
    grad_normed_attn = lax.psum_scatter(
        jnp.einsum("trc,tdc->rd", grad_project, w_qkv, preferred_element_type=jnp.float32).astype(
            jnp.bfloat16
        ),
        "head",
        scatter_dimension=0,
        tiled=True,
    ).astype(jnp.float32)
    grad_input_norm, grad_gain_attn, grad_shift_attn = norm_attn_pull(grad_normed_attn)
    grad_in = grad_resid + grad_input_norm
    grad_qkv_sum, grad_attn_sum = (
        sum_at_owner(grad_w_qkv.astype(jnp.bfloat16), "dp", 1),
        sum_at_owner(
            grad_w_attn.reshape(head_count, HEAD_DIM * width).astype(jnp.bfloat16), "dp", 1
        ),
    )
    summed_small = (
        lax.psum_scatter(grad_gain_attn, ("dp", "head"), scatter_dimension=0, tiled=True),
        lax.psum_scatter(grad_shift_attn, ("dp", "head"), scatter_dimension=0, tiled=True),
        lax.psum_scatter(grad_gain_moe, ("dp", "head"), scatter_dimension=0, tiled=True),
        lax.psum_scatter(grad_shift_moe, ("dp", "head"), scatter_dimension=0, tiled=True),
        lax.psum_scatter(grad_router, ("dp", "head"), scatter_dimension=0, tiled=True),
    )
    return (
        layer_out,
        grad_in,
        grad_qkv_sum,
        grad_attn_sum,
        summed_small[0],
        summed_small[1],
        summed_small[2],
        summed_small[3],
        summed_small[4],
        grad_w_in,
        grad_w_hidden,
    )


def tiles(n_dp, n_head, args):
    layer_in, w_attn, w_router = args[0], args[3], args[8]
    rows, width = layer_in.shape
    n = n_dp * n_head
    experts = w_router.shape[1]
    return (
        n_dp == 16
        and n_head == 2
        and experts == n
        and max(2, 3 * rows // experts) == 12
        and rows == 128
        and width % (8 * n) == 0
        and (width // n // 8) * 40 <= 128
        and experts + 4 <= 40
        and w_attn.shape[0] == width // 2
    )


def solution(mesh):
    placed = (
        P(("dp", "head"), None),
        P(("dp", "head"), None),
        P(None, None, "head"),
        P("head", None),
        P(),
        P(),
        P(),
        P(),
        P(),
        P(("dp", "head"), None, None),
        P(("dp", "head"), None, None),
        P(("dp", "head"), None),
        P("dp"),
        P(("dp", "head")),
    )
    n_dp, n_head = mesh.shape["dp"], mesh.shape["head"]

    def chosen(*args):
        if tiles(n_dp, n_head, args):
            return fast_body(n_dp, n_head, *args)
        return body(*args)

    return jax.shard_map(
        chosen,
        mesh=mesh,
        in_specs=placed,
        out_specs=(
            P(("dp", "head"), None),
            P(("dp", "head"), None),
            P(None, "dp", "head"),
            P("head", "dp"),
            P(("dp", "head")),
            P(("dp", "head")),
            P(("dp", "head")),
            P(("dp", "head")),
            P(("dp", "head"), None),
            P(("dp", "head"), None, None),
            P(("dp", "head"), None, None),
        ),
        check_vma=False,
    )
```
